32 devices in a mesh: dp: 4 (over x, core), fsdp: 8 (over z, y).
Axes of the slice: x: 2, y: 2, z: 4, core: 2. Of those that a mesh axis runs over, the one named last changes fastest.
Arguments:
- byte_inputs: bfloat16 [3, 32, 1024, 768], P(None, ('dp', 'fsdp')), may hold values from -60 to 60
- lengths: int32 [3, 32], P(None, ('dp', 'fsdp')), may hold values from 256 to 1024, as said below
- latent_array: bfloat16 [256, 1280], P(None, ('dp', 'fsdp')), may hold values from -6 to 6
- gain_bytes: bfloat16 [768], P(('dp', 'fsdp')), may hold values from 0.25 to 1.75
- bias_bytes: bfloat16 [768], P(('dp', 'fsdp')), may hold values from -1.5 to 1.5
- gain_latent: bfloat16 [1280], P(('dp', 'fsdp')), may hold values from 0.25 to 1.75
- bias_latent: bfloat16 [1280], P(('dp', 'fsdp')), may hold values from -1.5 to 1.5
- query_weight: bfloat16 [1280, 256], P(('dp', 'fsdp')), may hold values from -0.15625 to 0.15625
- key_weight: bfloat16 [768, 256], P(('dp', 'fsdp')), may hold values from -0.21875 to 0.21875
- value_weight: bfloat16 [768, 1280], P(('dp', 'fsdp')), may hold values from -0.21875 to 0.21875
- output_weight: bfloat16 [1280, 1280], P(('dp', 'fsdp')), may hold values from -2.5 to 2.5
- gain_feed: bfloat16 [1280], P(('dp', 'fsdp')), may hold values from 0.25 to 1.75
- bias_feed: bfloat16 [1280], P(('dp', 'fsdp')), may hold values from -1.5 to 1.5
- up_weight: bfloat16 [1280, 1280], P(('dp', 'fsdp')), may hold values from -0.15625 to 0.15625
- down_weight: bfloat16 [1280, 1280], P(('dp', 'fsdp')), may hold values from -0.15625 to 0.15625
- cotangent: bfloat16 [3, 32, 256, 1280], P(None, ('dp', 'fsdp')), may hold values from -6 to 6
Outputs:
- latents_out: bfloat16 [3, 32, 256, 1280], P(None, ('dp', 'fsdp'))
- grad_inputs: bfloat16 [3, 32, 1024, 768], P(None, ('dp', 'fsdp'))
- grad_latent_array: float32 [256, 1280], P(None, ('dp', 'fsdp'))
- grad_gain_bytes: float32 [768], P(('dp', 'fsdp'))
- grad_bias_bytes: float32 [768], P(('dp', 'fsdp'))
- grad_gain_latent: float32 [1280], P(('dp', 'fsdp'))
- grad_bias_latent: float32 [1280], P(('dp', 'fsdp'))
- grad_query: float32 [1280, 256], P(('dp', 'fsdp'))
- grad_key: float32 [768, 256], P(('dp', 'fsdp'))
- grad_value: float32 [768, 1280], P(('dp', 'fsdp'))
- grad_output: float32 [1280, 1280], P(('dp', 'fsdp'))
- grad_gain_feed: float32 [1280], P(('dp', 'fsdp'))
- grad_bias_feed: float32 [1280], P(('dp', 'fsdp'))
- grad_up: float32 [1280, 1280], P(('dp', 'fsdp'))
- grad_down: float32 [1280, 1280], P(('dp', 'fsdp'))
The draws below stay inside these ranges and needn't reach their ends.
Inputs may be any that keep to these rules, and one draw needn't show every extreme that they name: `lengths`: slots at or past a sequence's length are padding; in every micro-batch some sequence fills all 1024 slots.
All inputs are finite; a program needn't handle non-finite values.
Results may differ from the reference program's by a relative error of at most 0.012.
The reference program's roundings to bfloat16 on the way count: a program that leaves them out, or rounds other values in their place, can miss the bound.
Values may be sent and summed in bfloat16 or wider, within the bound.
No kernel may reach another device: no remote copies, remote signals or barrier semaphores. Data moves between devices by JAX's collectives and lax.ppermute only.
A program may use at most 192 MiB of HBM per device.

```python
import math
import jax
import jax.numpy as jnp
from jax import lax

D_IN = 768
D_LAT = 1280
NL = 256
QK = 256
V = 1280
HEADS = 8
SEQ = 1024
MB = 3
SEQS = 32


def draw_byte_inputs(key, part):
    first_key, second_key, third_key = jax.random.split(key, 3)
    full_shape = (MB, SEQS, SEQ, D_IN)
    columns = jnp.exp(jax.random.uniform(second_key, (D_IN,), jnp.float32, math.log(0.3), math.log(3.0)))
    row_scale = jnp.exp(jax.random.uniform(third_key, (MB, SEQS, SEQ, 1), jnp.float32, math.log(0.5), math.log(5.0)))
    base_draw = jnp.clip(jax.random.normal(first_key, full_shape, jnp.float32), -4.0, 4.0)
    return (base_draw * columns * row_scale).astype(jnp.bfloat16)


def draw_lengths(key, part):
    first_key, second_key = jax.random.split(key)
    drawn = jax.random.randint(first_key, (MB, SEQS), SEQ // 4, SEQ + 1, jnp.int32)
    fuller = jax.random.randint(second_key, (MB, 1), 0, SEQS, jnp.int32)
    places = lax.broadcasted_iota(jnp.int32, (MB, SEQS), 1)
    return jnp.where(places == fuller, SEQ, drawn).astype(jnp.int32)


def with_spikes(values, stream_key, source, target, shards_of, factor):
    def block_of(axis_at):
        return (jnp.arange(values.shape[axis_at]) // (values.shape[axis_at] // shards_of)).reshape((-1,) + (1,) * (values.ndim - 1 - axis_at))

    near = jax.random.permutation(stream_key, shards_of)[block_of(target)]
    second = (block_of(target) + shards_of // 2) % shards_of
    return jnp.where((block_of(source) == near) | (block_of(source) == second), factor * values, values)


def level_of(stream_key, dims, pieces, low, high):
    gain, own = 1.0, jax.random.fold_in(stream_key, 6)
    for axis_at, shards_of in pieces:
        heights = jnp.exp(jax.random.uniform(jax.random.fold_in(own, axis_at), (shards_of,), jnp.float32, low / len(pieces), high / len(pieces)))
        gain = gain * jnp.repeat(heights, dims[axis_at] // shards_of).reshape([-1 if axis == axis_at else 1 for axis in range(len(dims))])
    return gain


def scatter_about(key, extent, scale, bound, shards=(), held_as=jnp.bfloat16):
    factor_of = level_of(key, extent, shards, -0.22, 0.18) if shards else 1.0
    values = jax.random.normal(key, extent, jnp.float32) * scale * factor_of
    return jnp.minimum(jnp.maximum(values, -bound), bound).astype(held_as)


def bell_draw_with(own_key, dims, spread, reach, cuts, heavy, kind=jnp.bfloat16):
    array = spread * jax.random.normal(own_key, dims, jnp.float32)
    if cuts:
        array = array * level_of(own_key, dims, cuts, -0.22, 0.18)
    return jnp.clip(with_spikes(array, jax.random.fold_in(own_key, 3), *heavy), -reach, reach).astype(kind)


def setup_inputs(seed: int = 0) -> dict:
    streams_of = jax.random.split(jax.random.key(seed), 17)
    byte_inputs = draw_byte_inputs(jax.random.fold_in(streams_of[16], 71), 0)
    lengths = draw_lengths(jax.random.fold_in(streams_of[16], 71), 0)
    latent_array = scatter_about(streams_of[2], (NL, D_LAT), 1.0, 6.0, ((1, 32),))
    gain_bytes = jnp.clip(1.0 + 0.15 * jax.random.normal(streams_of[3], (D_IN,), jnp.float32), 0.25, 1.75).astype(jnp.bfloat16)
    bias_bytes = scatter_about(streams_of[4], (D_IN,), 0.3, 1.5, ((0, 32),))
    gain_latent = jnp.clip(1.0 + 0.15 * jax.random.normal(streams_of[5], (D_LAT,), jnp.float32), 0.25, 1.75).astype(jnp.bfloat16)
    bias_latent = scatter_about(streams_of[6], (D_LAT,), 0.3, 1.5, ((0, 32),))
    query_weight = scatter_about(streams_of[7], (D_LAT, QK), D_LAT ** -0.5, 0.15625, ((0, 32),))
    key_weight = scatter_about(streams_of[8], (D_IN, QK), D_IN ** -0.5, 0.21875, ((0, 32),))
    value_weight = scatter_about(streams_of[9], (D_IN, V), D_IN ** -0.5, 0.21875, ((0, 32),))
    output_weight = scatter_about(streams_of[10], (V, D_LAT), (4 * V // SEQ) ** -0.5, 2.5, ((0, 32),))
    gain_feed = jnp.clip(1.0 + 0.15 * jax.random.normal(streams_of[11], (D_LAT,), jnp.float32), 0.25, 1.75).astype(jnp.bfloat16)
    bias_feed = scatter_about(streams_of[12], (D_LAT,), 0.3, 1.5, ((0, 32),))
    up_weight = scatter_about(streams_of[13], (D_LAT, D_LAT), D_LAT ** -0.5, 0.15625, ((0, 32),))
    down_weight = scatter_about(streams_of[14], (D_LAT, D_LAT), D_LAT ** -0.5, 0.15625, ((0, 32),))
    cotangent = bell_draw_with(streams_of[15], (MB, SEQS, NL, D_LAT), 1.0, 6.0, ((1, 32),), (1, 3, 32, 2.75))
    return {"byte_inputs": byte_inputs, "lengths": lengths, "latent_array": latent_array, "gain_bytes": gain_bytes, "bias_bytes": bias_bytes, "gain_latent": gain_latent, "bias_latent": bias_latent, "query_weight": query_weight, "key_weight": key_weight, "value_weight": value_weight, "output_weight": output_weight, "gain_feed": gain_feed, "bias_feed": bias_feed, "up_weight": up_weight, "down_weight": down_weight, "cotangent": cotangent}


@jax.custom_vjp
def low(v):
    return lax.optimization_barrier(v.astype(jnp.bfloat16)).astype(jnp.float32)

@jax.custom_vjp
def low_back(v):
    return v

def low_keep(v):
    return (low(v), None)

def low_pass(kept, grad):
    return (grad,)

def back_keep(v):
    return (v, None)

def back_low(kept, grad):
    return (low(grad),)
low.defvjp(low_keep, low_pass)
low_back.defvjp(back_keep, back_low)
epsilon = 1e-05

def matmul(left_side, right_side):
    return jnp.dot(left_side, right_side, precision=lax.Precision.HIGHEST)

def normalize(source, gain_vector, bias_vector):
    average = lax.optimization_barrier(jnp.mean(source, axis=-1, keepdims=True))
    centered = source - average
    variance = lax.optimization_barrier(jnp.mean(centered * centered, axis=-1, keepdims=True))
    return centered * lax.rsqrt(variance + epsilon) * gain_vector + bias_vector

def forward(params, inputs, length):
    latent_array, gain_bytes, bias_bytes, gain_latent, bias_latent, query_weight, key_weight, value_weight, output_weight, gain_feed, bias_feed, up_weight, down_weight = params
    query_width = QK // HEADS
    value_width = V // HEADS
    factor = query_width ** (-0.5)
    bytes_low = low(normalize(inputs, gain_bytes, bias_bytes))
    key_rows = low_back(low(matmul(bytes_low, key_weight)))
    value_rows = low_back(low(matmul(bytes_low, value_weight)))
    latent_low = low(normalize(latent_array, gain_latent, bias_latent))
    queries = low_back(low(matmul(latent_low, query_weight)))
    query_heads = queries.reshape(NL, HEADS, query_width)
    key_heads = key_rows.reshape(SEQ, HEADS, query_width)
    value_heads = value_rows.reshape(SEQ, HEADS, value_width)
    scores = low_back(jnp.einsum('nhd,shd->hns', query_heads, key_heads, precision=lax.Precision.HIGHEST) * factor)
    live_mask = jnp.arange(SEQ) < length
    scores = jnp.where(live_mask[None, None, :], scores, -1e+30)
    probability = jax.nn.softmax(scores, axis=-1)
    mixed_rows = jnp.einsum('hns,shd->nhd', low(probability), value_heads, precision=lax.Precision.HIGHEST)
    mixed_rows = low_back(low(mixed_rows.reshape(NL, V)))
    first_sum = latent_array + low_back(matmul(mixed_rows, output_weight))
    middle_low = low(normalize(first_sum, gain_feed, bias_feed))
    upper_rows = low_back(matmul(middle_low, up_weight))
    hidden = low(jax.nn.gelu(upper_rows, approximate=False))
    return first_sum + low_back(matmul(hidden, down_weight))

def reference(byte_inputs, lengths, latent_array, gain_bytes, bias_bytes, gain_latent, bias_latent, query_weight, key_weight, value_weight, output_weight, gain_feed, bias_feed, up_weight, down_weight, cotangent):
    params = tuple((weight.astype(jnp.float32) for weight in (latent_array, gain_bytes, bias_bytes, gain_latent, bias_latent, query_weight, key_weight, value_weight, output_weight, gain_feed, bias_feed, up_weight, down_weight)))
    sequence_count = MB * SEQS
    flat_inputs = byte_inputs.reshape(sequence_count, SEQ, D_IN).astype(jnp.float32)
    flat_lengths = lengths.reshape(sequence_count)
    flat_cotangent = cotangent.reshape(sequence_count, NL, D_LAT).astype(jnp.float32)

    def one_sequence(totals, sequence_item):
        inputs, length, cotangent_row = sequence_item
        result, pullback = jax.vjp(lambda weights, source: forward(weights, source, length), params, inputs)
        grad_params, grad_source = pullback(cotangent_row)
        totals = jax.tree.map(jnp.add, totals, grad_params)
        return (totals, (result.astype(jnp.bfloat16), grad_source.astype(jnp.bfloat16)))
    empty_sums = jax.tree.map(jnp.zeros_like, params)
    totals, (outputs, input_grads) = lax.scan(one_sequence, empty_sums, (flat_inputs, flat_lengths, flat_cotangent))
    grad_latent, grad_gain_bytes, grad_bias_bytes, grad_gain_latent, grad_bias_latent, grad_query, grad_key, grad_value, grad_output, grad_gain_feed, grad_bias_feed, grad_up, grad_down = totals
    return (outputs.reshape(MB, SEQS, NL, D_LAT), input_grads.reshape(MB, SEQS, SEQ, D_IN), grad_latent, grad_gain_bytes, grad_bias_bytes, grad_gain_latent, grad_bias_latent, grad_query, grad_key, grad_value, grad_output, grad_gain_feed, grad_bias_feed, grad_up, grad_down)
```

```python
import jax
import jax.numpy as jnp
from jax import lax
from jax.sharding import PartitionSpec as P

NL = 256
QK = 256
V = 1280
HEADS = 8
MB = 3
AXES = ("dp", "fsdp")
epsilon = 1e-05


class Plan:
    def __init__(self, mesh):
        self.count = mesh.shape["dp"] * mesh.shape["fsdp"]
        self.core = mesh.shape["fsdp"].bit_length() - 1
        far, near, others = self.core + 1, 0, list(range(1, self.core))
        self.orders = (others + [near, far], others + [far, near])
        self.steps = len(self.orders[0])
        self.half = self.count // 2

    def core_of(self, index):
        return (index >> self.core) & 1

    def pairs(self, step):
        if step == self.steps:
            return [(i, i ^ (1 << self.core)) for i in range(self.count)]
        return [(i, i ^ (1 << self.orders[self.core_of(i)][step])) for i in range(self.count)]

    def me(self):
        return lax.axis_index("dp") * (1 << self.core) + lax.axis_index("fsdp")

    def bit(self, me, step):
        first, second = (order[step] for order in self.orders)
        return jnp.where(self.core_of(me) == 0, me >> first, me >> second) & 1

    def place(self, index, order):
        return sum(((index >> bit) & 1) << step for step, bit in enumerate(order))

    def gather_table(self, me):
        apart = jnp.arange(self.count, dtype=jnp.int32) ^ me
        own, other = (self.place(apart, order) for order in self.orders)
        swap = self.core_of(apart) ^ self.core_of(me)
        return jnp.where(swap == 0, own, other) + self.half * self.core_of(apart)


def permute(block, pairs):
    return lax.ppermute(block, AXES, pairs)


def gather_rows(plan, shard):
    block = shard[None]
    for step in range(plan.steps):
        block = jnp.concatenate([block, permute(block, plan.pairs(step))])
    return jnp.concatenate([block, permute(block, plan.pairs(plan.steps))])


def scatter_order(plan, grad):
    rows = grad.shape[0] // plan.count
    middle = plan.half // 4
    view = grad.astype(jnp.bfloat16).reshape(2, 2, middle, 2, rows, -1)
    first = view[:, 0].transpose(0, 2, 1, 3, 4)
    second = view[:, 1].transpose(2, 0, 1, 3, 4)
    return jnp.stack([first, second]).reshape(2, plan.half, rows, -1)


def scatter_rows(plan, blocks):
    me = plan.me()
    keep_at = plan.core_of(me)
    for step in range(plan.steps, -1, -1):
        send = lax.dynamic_index_in_dim(blocks, 1 - keep_at, 0, keepdims=False)
        keep = lax.dynamic_index_in_dim(blocks, keep_at, 0, keepdims=False)
        got = permute(send, plan.pairs(step))
        total = keep.astype(jnp.float32) + got.astype(jnp.float32)
        if step == 0:
            return total[0]
        blocks = total.astype(jnp.bfloat16).reshape((2, -1) + total.shape[1:])
        keep_at = plan.bit(me, step - 1)


def normalize(source, gain_vector, bias_vector):
    average = jnp.mean(source, axis=-1, keepdims=True)
    centered = source - average
    variance = jnp.mean(centered * centered, axis=-1, keepdims=True)
    return centered * lax.rsqrt(variance + epsilon) * gain_vector + bias_vector


def gelu_exact(upper_rows):
    return jax.nn.gelu(upper_rows, approximate=False)


def dot(left_side, right_side):
    return jnp.dot(left_side, right_side, preferred_element_type=jnp.float32)


def outer_sum(left_side, right_side):
    return jnp.einsum("rd,rf->df", left_side, right_side, preferred_element_type=jnp.float32)


def back_dot(left_side, right_side):
    return jnp.einsum("rf,df->rd", left_side, right_side, preferred_element_type=jnp.float32)


def attention_scores(query_heads, key_heads, length, factor):
    scores = (
        jnp.einsum("nhd,shd->hns", query_heads, key_heads, preferred_element_type=jnp.float32)
        * factor
    )
    live_mask = lax.iota(jnp.int32, key_heads.shape[0]) < length
    return jnp.where(live_mask[None, None, :], scores, -1e30)


def per_device(plan, byte_inputs, lengths, latent_array, gain_bytes, bias_bytes, gain_latent, bias_latent,
               query_weight, key_weight, value_weight, output_weight, gain_feed, bias_feed, up_weight,
               down_weight, cotangent):
    query_width = QK // HEADS
    value_width = V // HEADS
    factor = query_width ** (-0.5)
    me = plan.me()
    table = plan.gather_table(me)

    def whole(shard):
        return jnp.take(gather_rows(plan, shard), table, axis=0).reshape(-1, shard.shape[1])

    def columns(*vectors):
        return jnp.pad(jnp.stack(vectors, axis=1), ((0, 0), (0, 128 - len(vectors))))

    byte_group = whole(jnp.concatenate([key_weight, value_weight, columns(gain_bytes, bias_bytes)], axis=1))
    latent_group = whole(jnp.concatenate(
        [query_weight, latent_array.T, columns(gain_latent, bias_latent, gain_feed, bias_feed)], axis=1))
    full_output = whole(output_weight)
    full_up = whole(up_weight)
    full_down = whole(down_weight)
    full_key, full_value = byte_group[:, :QK], byte_group[:, QK:QK + V]
    byte_vectors = byte_group[:, QK + V:QK + V + 2].T.astype(jnp.float32)
    full_query = latent_group[:, :QK]
    latent_float = latent_group[:, QK:QK + NL].T.astype(jnp.float32)
    latent_vectors = latent_group[:, QK + NL:QK + NL + 4].T.astype(jnp.float32)

    inputs = byte_inputs[:, 0].astype(jnp.float32)
    slots = inputs.shape[1]
    inputs = inputs.reshape(MB * slots, -1)
    normed_bytes, pull_bytes = jax.vjp(normalize, inputs, byte_vectors[0], byte_vectors[1])
    bytes_low = normed_bytes.astype(jnp.bfloat16)
    key_rows = dot(bytes_low, full_key).astype(jnp.bfloat16)
    value_rows = dot(bytes_low, full_value).astype(jnp.bfloat16)
    normed_latent, pull_latent = jax.vjp(normalize, latent_float, latent_vectors[0], latent_vectors[1])
    latent_low = normed_latent.astype(jnp.bfloat16)
    queries = dot(latent_low, full_query).astype(jnp.bfloat16)
    query_heads = queries.reshape(NL, HEADS, query_width)
    key_heads = key_rows.reshape(MB, slots, HEADS, query_width)
    value_heads = value_rows.reshape(MB, slots, HEADS, value_width)
    saved = []
    mixed = []
    for m in range(MB):
        scores = attention_scores(query_heads, key_heads[m], lengths[m, 0], factor)
        probability = jax.nn.softmax(scores, axis=-1)
        saved.append(probability)
        mixed.append(jnp.einsum("hns,shd->nhd", probability.astype(jnp.bfloat16), value_heads[m],
                                preferred_element_type=jnp.float32).reshape(NL, V).astype(jnp.bfloat16))
    mixed_rows = jnp.concatenate(mixed)
    first_sum = jnp.tile(latent_float, (MB, 1)) + dot(mixed_rows, full_output)
    normed_middle, pull_middle = jax.vjp(normalize, first_sum, latent_vectors[2], latent_vectors[3])
    middle_low = normed_middle.astype(jnp.bfloat16)
    upper_rows = dot(middle_low, full_up)
    hidden_float, pull_gelu = jax.vjp(gelu_exact, upper_rows)
    hidden = hidden_float.astype(jnp.bfloat16)
    latents_out = (first_sum + dot(hidden, full_down)).astype(jnp.bfloat16).reshape(MB, 1, NL, -1)

    down_low = cotangent[:, 0].reshape(MB * NL, -1)
    cotangent_rows = down_low.astype(jnp.float32)
    grad_down = scatter_rows(plan, scatter_order(plan, outer_sum(hidden, down_low)))
    (upper_grad,) = pull_gelu(back_dot(down_low, full_down))
    upper_low = upper_grad.astype(jnp.bfloat16)
    grad_up = scatter_rows(plan, scatter_order(plan, outer_sum(middle_low, upper_low)))
    first_extra, grad_gain_feed, grad_bias_feed = pull_middle(back_dot(upper_low, full_up))
    first_grad = cotangent_rows + first_extra
    attend_low = first_grad.astype(jnp.bfloat16)
    grad_output = scatter_rows(plan, scatter_order(plan, outer_sum(mixed_rows, attend_low)))
    mixed_grad = back_dot(attend_low, full_output).astype(jnp.bfloat16).reshape(MB, NL, HEADS, value_width)
    value_grads, key_grads, query_total = [], [], 0.0
    for m in range(MB):
        probability = saved[m]
        weight_grad = jnp.einsum("nhd,shd->hns", mixed_grad[m], value_heads[m], preferred_element_type=jnp.float32)
        value_grads.append(jnp.einsum("hns,nhd->shd", probability.astype(jnp.bfloat16), mixed_grad[m],
                                      preferred_element_type=jnp.float32).reshape(-1, V).astype(jnp.bfloat16))
        score_low = (probability * (weight_grad - jnp.sum(weight_grad * probability, axis=-1, keepdims=True))
                     ).astype(jnp.bfloat16)
        query_grad = jnp.einsum("hns,shd->nhd", score_low, key_heads[m], preferred_element_type=jnp.float32) * factor
        query_total = query_total + query_grad.reshape(NL, QK).astype(jnp.bfloat16).astype(jnp.float32)
        key_grad = jnp.einsum("hns,nhd->shd", score_low, query_heads, preferred_element_type=jnp.float32) * factor
        key_grads.append(key_grad.reshape(-1, QK).astype(jnp.bfloat16))
    value_grad = jnp.concatenate(value_grads)
    key_grad = jnp.concatenate(key_grads)
    source_grad = back_dot(key_grad, full_key) + back_dot(value_grad, full_value)
    input_extra, grad_gain_bytes, grad_bias_bytes = pull_bytes(source_grad)
    grad_inputs = input_extra.astype(jnp.bfloat16).reshape(MB, 1, slots, -1)
    byte_grads = scatter_rows(plan, scatter_order(plan, jnp.concatenate(
        [outer_sum(bytes_low, key_grad), outer_sum(bytes_low, value_grad), columns(grad_gain_bytes, grad_bias_bytes)],
        axis=1)))
    query_low = query_total.astype(jnp.bfloat16)
    latent_extra, grad_gain_latent, grad_bias_latent = pull_latent(back_dot(query_low, full_query))
    grad_latent = first_grad.reshape(MB, NL, -1).sum(0) + latent_extra
    latent_grads = scatter_rows(plan, scatter_order(plan, jnp.concatenate(
        [outer_sum(latent_low, query_low), grad_latent.T,
         columns(grad_gain_latent, grad_bias_latent, grad_gain_feed, grad_bias_feed)], axis=1)))
    latent_columns = latent_grads[:, QK + NL:]
    byte_columns = byte_grads[:, QK + V:]
    return (latents_out, grad_inputs, latent_grads[:, QK:QK + NL].T, byte_columns[:, 0], byte_columns[:, 1],
            latent_columns[:, 0], latent_columns[:, 1], latent_grads[:, :QK], byte_grads[:, :QK],
            byte_grads[:, QK:QK + V], grad_output, latent_columns[:, 2], latent_columns[:, 3], grad_up, grad_down)


def solution(mesh):
    plan = Plan(mesh)
    rows, lane, lanes = P(AXES, None), P(AXES), P(None, AXES)
    batch = P(None, AXES, None, None)
    return jax.shard_map(
        lambda *arrays: per_device(plan, *arrays),
        mesh=mesh,
        in_specs=(batch, lanes, lanes, lane, lane, lane, lane, rows, rows, rows, rows, lane, lane, rows, rows, batch),
        out_specs=(batch, batch, lanes, lane, lane, lane, lane, rows, rows, rows, rows, lane, lane, rows, rows),
        check_vma=False,
    )
```
